32 devices in a mesh: tissue: 2 (over x), sample: 4 (over y, core), variant: 4 (over z).
Axes of the slice: x: 2, y: 2, z: 4, core: 2. Of those that a mesh axis runs over, the one named last changes fastest.
Arguments:
- dosage: bfloat16 [52, 512, 512], P('tissue', 'sample', 'variant'), may hold values from 0 to 2
- express: bfloat16 [52, 512, 2048], P('tissue', 'sample', 'variant'), may hold values from -6 to 6
- covar: float32 [52, 32, 512], P('tissue', None, 'sample'), may hold values from -6 to 6
- member: int32 [52, 512], P('tissue', 'sample'), may hold values 0 or 1
- live: int32 [52], replicated, may hold values 0 or 1
- mixing: float32 [52, 52], replicated, may hold values from -1 to 2, as said below
Outputs:
- chi_stat: float32 [512, 2048], P('variant', 'sample')
- meta_stat: float32 [512, 2048], P('variant', 'sample')
The draws below stay inside these ranges and needn't reach their ends.
Inputs may be any that keep to these rules, and one draw needn't show every extreme that they name: mixing is the identity plus a dense spread of off-diagonal and diagonal terms.
All inputs are finite; a program needn't handle non-finite values. No bound on the sum of `member` on one device may be relied on, other than what follows from the above.
Results may differ from the reference program's by a relative error of at most 0.019.
Values may be sent and summed in bfloat16 or wider, within the bound.
A program may use at most 128 MiB of HBM per device.

```python
import jax
import jax.numpy as jnp
from jax import lax

S_DEV = 128
V_DEV = 128
GENES = 2048
K = 32
TISSUES = 52
SAMPLES = 512
VARIANTS = 512
N_SAMPLE = 4


def draw_mixing(key, part):
    noise = jnp.clip(jax.random.normal(key, (TISSUES, TISSUES), jnp.float32), -3.0, 3.0)
    return jnp.eye(TISSUES, dtype=jnp.float32) + 0.35 * noise / jnp.sqrt(jnp.float32(TISSUES))


def with_ends(drawn, key, low, top_value):
    spot = [jax.random.randint(jax.random.fold_in(key, axis), (), 0, length) for axis, length in enumerate(drawn.shape)]
    main_axis = drawn.shape.index(max(drawn.shape))
    neighbour = spot[:main_axis] + [(spot[main_axis] + 1) % drawn.shape[main_axis]] + spot[main_axis + 1:]
    return drawn.at[tuple(spot)].set(low).at[tuple(neighbour)].set(top_value)


def steps_of(key, dims, pieces, least, top_value):
    loudness, own = 1.0, jax.random.fold_in(key, 6)
    for position, parts in pieces:
        heights = jnp.exp(jax.random.uniform(jax.random.fold_in(own, position), (parts,), jnp.float32, least / len(pieces), top_value / len(pieces)))
        loudness = loudness * jnp.repeat(heights, dims[position] // parts).reshape([-1 if axis == position else 1 for axis in range(len(dims))])
    return loudness


def bell_draw(key, dims, scale, reach, pieces=(), held_as=jnp.bfloat16):
    drawn = jax.random.normal(key, dims, jnp.float32) * scale
    if len(pieces) > 0:
        drawn = steps_of(key, dims, pieces, -0.22, 0.18) * drawn
    return jnp.clip(drawn, min=-reach, max=reach).astype(held_as)


def setup_inputs(seed: int = 0) -> dict:
    keys = jax.random.split(jax.random.key(seed), 7)
    return {
        "dosage": jnp.clip(2.0 * jax.random.uniform(keys[0], (TISSUES, SAMPLES, VARIANTS), jnp.float32) ** steps_of(keys[0], (TISSUES, SAMPLES, VARIANTS), ((0, 2), (1, 4), (2, 4)), -0.2, 0.2), 0.0, 2.0).astype(jnp.bfloat16),
        "express": bell_draw(keys[1], (TISSUES, SAMPLES, GENES), 1.0, 6.0, ((0, 2), (1, 4), (2, 4))),
        "covar": bell_draw(keys[2], (TISSUES, K, SAMPLES), 1.0, 6.0, ((0, 2), (2, 4)), jnp.float32),
        "member": with_ends((jax.random.randint(keys[3], (TISSUES, SAMPLES), 0, 16) < 11).astype(jnp.int32), jax.random.fold_in(keys[3], 1), 0, 1),
        "live": with_ends((jax.random.randint(keys[4], (TISSUES,), 0, 16) < 15).astype(jnp.int32), jax.random.fold_in(keys[4], 1), 0, 1),
        "mixing": draw_mixing(jax.random.fold_in(keys[6], 71), 0),
    }


def reference(dosage, express, covar, member, live, mixing):
    highest = lax.Precision.HIGHEST
    weights = member.astype(jnp.float32)
    dos_masked = dosage.astype(jnp.float32) * weights[:, :, None]
    exp_masked = express.astype(jnp.float32) * weights[:, :, None]
    cov_masked = covar * weights[:, None, :]
    gram_sum = jnp.einsum('tks,tjs->tkj', cov_masked, cov_masked, precision=highest) + jnp.eye(K, dtype=jnp.float32)
    amat_sum = jnp.einsum('tks,tsv->tkv', cov_masked, dos_masked, precision=highest)
    bmat_sum = jnp.einsum('tks,tsg->tkg', cov_masked, exp_masked, precision=highest)
    counts = lax.optimization_barrier(jnp.sum(weights, axis=1))
    gsq_sum = lax.optimization_barrier(jnp.sum(dos_masked * dos_masked, axis=1))
    esq_sum = lax.optimization_barrier(jnp.sum(exp_masked * exp_masked, axis=1))
    proj_dos = jnp.linalg.solve(gram_sum, amat_sum)
    proj_exp = jnp.linalg.solve(gram_sum, bmat_sum)
    gres = (dos_masked - jnp.einsum('tks,tkv->tsv', cov_masked, proj_dos, precision=highest)).astype(jnp.bfloat16)
    eres = (exp_masked - jnp.einsum('tks,tkg->tsg', cov_masked, proj_exp, precision=highest)).astype(jnp.bfloat16)
    gnorm = gsq_sum - lax.optimization_barrier(jnp.sum(amat_sum * proj_dos, axis=1))
    enorm = esq_sum - lax.optimization_barrier(jnp.sum(bmat_sum * proj_exp, axis=1))
    live_f = live.astype(jnp.float32)
    scales = live_f * jnp.sqrt(jnp.maximum(counts - K, 1.0))
    inv_gene = 1.0 / jnp.sqrt(enorm + 1e-05)
    nlive = jnp.maximum(jnp.sum(live_f), 1.0)
    tissues = dosage.shape[0]
    exp_blocks = eres.astype(jnp.float32).reshape(tissues, N_SAMPLE, S_DEV, GENES)
    nblocks = dosage.shape[2] // V_DEV

    def one_block(index):
        start = (index * V_DEV).astype(jnp.int32)
        dos_block = lax.dynamic_slice_in_dim(gres, start, V_DEV, 2).astype(jnp.float32)
        dos_block = dos_block.reshape(tissues, N_SAMPLE, S_DEV, V_DEV)
        partial_value = jnp.einsum('tbsv,tbsg->btvg', dos_block, exp_blocks)
        partial_value = lax.optimization_barrier(partial_value.astype(jnp.bfloat16)).astype(jnp.float32)
        cross = lax.optimization_barrier(jnp.sum(partial_value, axis=0))
        inv_var = 1.0 / jnp.sqrt(lax.dynamic_slice_in_dim(gnorm, start, V_DEV, 1) + 1e-05)
        zvals = scales[:, None, None] * cross * inv_var[:, :, None] * inv_gene[:, None, :]
        mixed = jnp.einsum('ut,tvg->uvg', mixing, zvals, precision=highest) * live_f[:, None, None]
        return (lax.optimization_barrier(jnp.sum(mixed * mixed, axis=0)) / nlive, lax.optimization_barrier(jnp.sum(mixed, axis=0)) / jnp.sqrt(nlive))
    chi_all, meta_all = lax.map(one_block, jnp.arange(nblocks, dtype=jnp.int32))
    variants = dosage.shape[2]
    return (chi_all.reshape(variants, GENES), meta_all.reshape(variants, GENES))
```

```python
import jax
import jax.numpy as jnp
from jax import lax
from jax.experimental import pallas as pl
from jax.experimental.pallas import tpu as pltpu
from jax.sharding import PartitionSpec as P

HIGHEST = lax.Precision.HIGHEST


def invert_kernel(gram_ref, out_ref):
    n = gram_ref.shape[0]
    lanes = gram_ref.shape[2]
    eye = (
        lax.broadcasted_iota(jnp.int32, (n, n, lanes), 0)
        == lax.broadcasted_iota(jnp.int32, (n, n, lanes), 1)
    ).astype(jnp.float32)
    out_ref[...] = gram_ref[...] + eye
    row_ids = lax.broadcasted_iota(jnp.int32, (n, lanes), 0)

    def step(k, carry):
        pivot = 1.0 / out_ref[k, pl.ds(k, 1), :]
        here = row_ids == k
        row = jnp.where(here, pivot, out_ref[k] * pivot)
        col = out_ref[:, pl.ds(k, 1), :]
        out_ref[...] = jnp.where(here[None], 0.0, out_ref[...]) - col * row[None]
        out_ref[k] = row
        return carry

    lax.fori_loop(0, n, step, 0)


def invert(gram):
    tis, n, _ = gram.shape
    lanes = -(-tis // 128) * 128
    packed = jnp.pad(jnp.transpose(gram, (1, 2, 0)), ((0, 0), (0, 0), (0, lanes - tis)))
    out = pl.pallas_call(
        invert_kernel,
        out_shape=jax.ShapeDtypeStruct((n, n, lanes), jnp.float32),
        name="invert_gram",
    )(packed)
    return jnp.transpose(out[:, :, :tis], (2, 0, 1))


def body(dosage, express, covar, member, live, mixing):
    tis_dev = dosage.shape[0]
    n_cov = covar.shape[1]
    n_x = lax.axis_size("tissue")
    n_s = lax.axis_size("sample")
    n_v = lax.axis_size("variant")
    ix = lax.axis_index("tissue")
    i_s = lax.axis_index("sample")
    i_v = lax.axis_index("variant")
    weights = member.astype(jnp.float32)
    dos_m = dosage.astype(jnp.float32) * weights[:, :, None]
    cov_m = covar * weights[:, None, :]
    exp_m = express.astype(jnp.float32) * weights[:, :, None]
    parts = (
        jnp.einsum("tks,tjs->tkj", cov_m, cov_m, precision=HIGHEST),
        jnp.einsum("tks,tsv->tkv", cov_m, dos_m, precision=HIGHEST),
        jnp.einsum("tks,tsg->tkg", cov_m, exp_m, precision=HIGHEST),
        jnp.sum(dos_m * dos_m, axis=1),
        jnp.sum(exp_m * exp_m, axis=1),
        jnp.sum(weights, axis=1),
    )
    gram, amat, bmat, gsq, esq, counts = (
        part.astype(jnp.float32)
        for part in lax.psum(tuple(part.astype(jnp.bfloat16) for part in parts), "sample")
    )
    inverse = invert(gram)
    pa = jnp.einsum("tkj,tjv->tkv", inverse, amat, precision=HIGHEST)
    pb = jnp.einsum("tkj,tjg->tkg", inverse, bmat, precision=HIGHEST)
    gnorm = gsq - jnp.sum(amat * pa, axis=1)
    enorm = esq - jnp.sum(bmat * pb, axis=1)
    live_f = live.astype(jnp.float32)
    live_own = lax.dynamic_slice_in_dim(live_f, ix * tis_dev, tis_dev, 0)
    scales = live_own * jnp.sqrt(jnp.maximum(counts - n_cov, 1.0))
    inv_var = 1.0 / jnp.sqrt(gnorm + 1e-05)
    inv_gene = scales[:, None] / jnp.sqrt(enorm + 1e-05)
    gres = dos_m - jnp.einsum("tks,tkv->tsv", cov_m, pa, precision=HIGHEST)
    gres = (gres * inv_var[:, None, :]).astype(jnp.bfloat16)
    eres = exp_m - jnp.einsum("tks,tkg->tsg", cov_m, pb, precision=HIGHEST)
    eres = (eres * inv_gene[:, None, :]).astype(jnp.bfloat16)
    gathered = lax.all_gather(gres, "variant", axis=0)
    part = jnp.einsum(
        "ntsv,tsg->ntvg", gathered, eres, preferred_element_type=jnp.float32
    ).astype(jnp.bfloat16)
    part = part.reshape((n_v * tis_dev,) + part.shape[2:])
    zvals = lax.psum_scatter(part, "sample", scatter_dimension=0, tiled=True)
    zvals = zvals.reshape((n_v // n_s, tis_dev) + zvals.shape[1:])
    rows = zvals.shape[2]
    half = rows // n_x
    kept = lax.dynamic_slice_in_dim(zvals, ix * half, half, 2)
    sent = lax.dynamic_slice_in_dim(zvals, (n_x - 1 - ix) * half, half, 2)
    got = lax.ppermute(sent, "tissue", [(0, 1), (1, 0)])
    mix_own = lax.dynamic_slice_in_dim(mixing, ix * tis_dev, tis_dev, 1)
    mix_far = lax.dynamic_slice_in_dim(mixing, (n_x - 1 - ix) * tis_dev, tis_dev, 1)
    yvals = jnp.einsum(
        "ut,mtvg->umvg",
        jnp.concatenate([mix_own, mix_far], axis=1) * live_f[:, None],
        jnp.concatenate([kept, got], axis=1).astype(jnp.float32),
        precision=HIGHEST,
    )
    nlive = jnp.maximum(jnp.sum(live_f), 1.0)
    stats = jnp.stack(
        [jnp.sum(yvals * yvals, axis=0) / nlive, jnp.sum(yvals, axis=0) / jnp.sqrt(nlive)]
    ).astype(jnp.bfloat16)
    if n_s == n_v:
        near, far = [], []
        for x in range(n_x):
            for i in range(n_s):
                for j in range(n_v):
                    source = (x * n_s + i) * n_v + j
                    near.append((source, (x * n_s + j) * n_v + i))
                    far.append((source, ((n_x - 1 - x) * n_s + j) * n_v + i))
        axes = ("tissue", "sample", "variant")
        one = lax.ppermute(stats[:, 0], axes, near)
        two = lax.ppermute(stats[:, 0], axes, far)
        full = jnp.concatenate(
            [jnp.where(ix == 0, one, two), jnp.where(ix == 0, two, one)], axis=1
        )
    else:
        blocks = lax.all_gather(stats, ("tissue", "sample", "variant"), axis=0)
        blocks = blocks.reshape((n_x, n_s, n_v) + stats.shape)
        blocks = jnp.transpose(blocks, (3, 1, 4, 0, 5, 2, 6))
        whole = blocks.reshape(2, n_v * rows, n_v * stats.shape[3])
        genes = whole.shape[2] // n_s
        full = lax.dynamic_slice(whole, (0, i_v * rows, i_s * genes), (2, rows, genes))
    full = full.astype(jnp.float32)
    return (full[0], full[1])


def solution(mesh):
    return jax.shard_map(
        body,
        mesh=mesh,
        in_specs=(
            P("tissue", "sample", "variant"),
            P("tissue", "sample", "variant"),
            P("tissue", None, "sample"),
            P("tissue", "sample"),
            P(),
            P(),
        ),
        out_specs=(P("variant", "sample"), P("variant", "sample")),
        check_vma=False,
    )
```

```python
import jax
import jax.numpy as jnp
from jax import lax
from jax.experimental import pallas as pl
from jax.experimental.pallas import tpu as pltpu
from jax.sharding import PartitionSpec as P

HIGHEST = lax.Precision.HIGHEST
CUTS = (0, 8, 17, 26)


def invert_kernel(gram_ref, out_ref):
    n = gram_ref.shape[0]
    lanes = gram_ref.shape[2]
    eye = (
        lax.broadcasted_iota(jnp.int32, (n, n, lanes), 0)
        == lax.broadcasted_iota(jnp.int32, (n, n, lanes), 1)
    ).astype(jnp.float32)
    out_ref[...] = gram_ref[...] + eye
    row_ids = lax.broadcasted_iota(jnp.int32, (n, lanes), 0)

    def step(k, carry):
        pivot = 1.0 / out_ref[k, pl.ds(k, 1), :]
        here = row_ids == k
        row = jnp.where(here, pivot, out_ref[k] * pivot)
        col = out_ref[:, pl.ds(k, 1), :]
        out_ref[...] = jnp.where(here[None], 0.0, out_ref[...]) - col * row[None]
        out_ref[k] = row
        return carry

    lax.fori_loop(0, n, step, 0)


def invert(gram):
    tis, n, _ = gram.shape
    lanes = -(-tis // 128) * 128
    packed = jnp.pad(jnp.transpose(gram, (1, 2, 0)), ((0, 0), (0, 0), (0, lanes - tis)))
    out = pl.pallas_call(
        invert_kernel,
        out_shape=jax.ShapeDtypeStruct((n, n, lanes), jnp.float32),
        name="invert_gram",
    )(packed)
    return jnp.transpose(out[:, :, :tis], (2, 0, 1))


def swap(value, bit, n_s):
    return lax.ppermute(value, "sample", [(i, i ^ bit) for i in range(n_s)])


def add(first, second):
    return (first.astype(jnp.float32) + second.astype(jnp.float32)).astype(jnp.bfloat16)


def sum_over_samples(value, n_s, i_s):
    half = value.shape[0] // 2
    odd = i_s % 2
    mine = lax.dynamic_slice_in_dim(value, odd * half, half, 0)
    sent = lax.dynamic_slice_in_dim(value, (1 - odd) * half, half, 0)
    mine = add(mine, swap(sent, 1, n_s))
    bit = 2
    while bit < n_s:
        mine = add(mine, swap(mine, bit, n_s))
        bit *= 2
    other = swap(mine, 1, n_s)
    return jnp.concatenate(
        [jnp.where(odd == 0, mine, other), jnp.where(odd == 0, other, mine)], axis=0
    )


def cross_chunk(gres, eres, n_s, n_v, i_s, i_v):
    if n_v == n_s:
        gathered = jnp.stack(
            [gres]
            + [
                lax.ppermute(gres, "variant", [(j, j ^ shift) for j in range(n_v)])
                for shift in range(1, n_v)
            ]
        )
        first = i_v
    else:
        gathered = lax.all_gather(gres, "variant", axis=0)
        first = 0
    per = n_v // n_s
    blocks = {}
    for offset in reversed(range(n_s)):
        pieces = [
            jnp.einsum(
                "tsv,tsg->tvg",
                lax.dynamic_index_in_dim(gathered, ((i_s ^ offset) * per + m) ^ first, 0, False),
                eres,
                preferred_element_type=jnp.float32,
            ).astype(jnp.bfloat16)
            for m in range(per)
        ]
        blocks[offset] = pieces[0] if per == 1 else jnp.concatenate(pieces, axis=1)
    bit = 1
    while bit < n_s:
        for offset in [o for o in blocks if o & bit]:
            arrived = swap(blocks.pop(offset), bit, n_s)
            blocks[offset ^ bit] = add(blocks[offset ^ bit], arrived)
        bit *= 2
    return blocks[0]


def body(dosage, express, covar, member, live, mixing):
    tis_dev = dosage.shape[0]
    n_cov = covar.shape[1]
    n_x = lax.axis_size("tissue")
    n_s = lax.axis_size("sample")
    n_v = lax.axis_size("variant")
    ix = lax.axis_index("tissue")
    i_s = lax.axis_index("sample")
    i_v = lax.axis_index("variant")
    weights = member.astype(jnp.float32)
    dos_m = dosage.astype(jnp.float32) * weights[:, :, None]
    cov_m = covar * weights[:, None, :]
    exp_m = express.astype(jnp.float32) * weights[:, :, None]
    gram = jnp.einsum("tks,tjs->tkj", cov_m, cov_m, precision=HIGHEST)
    amat = jnp.einsum("tks,tsv->tkv", cov_m, dos_m, precision=HIGHEST)
    bmat = jnp.einsum("tks,tsg->tkg", cov_m, exp_m, precision=HIGHEST)
    gsq = jnp.sum(dos_m * dos_m, axis=1)
    esq = jnp.sum(exp_m * exp_m, axis=1)
    counts = jnp.sum(weights, axis=1)
    n_var, n_gene = dosage.shape[2], express.shape[2]
    count_row = jnp.pad(counts[:, None], ((0, 0), (0, n_cov - 1)))
    packed = jnp.concatenate(
        [
            jnp.concatenate([bmat, amat, gram], axis=2).astype(jnp.bfloat16),
            jnp.concatenate([esq, gsq, count_row], axis=1).astype(jnp.bfloat16)[:, None],
        ],
        axis=1,
    )
    packed = sum_over_samples(packed, n_s, i_s).astype(jnp.float32)
    bmat, esq = packed[:, :n_cov, :n_gene], packed[:, n_cov, :n_gene]
    amat, gsq = (
        packed[:, :n_cov, n_gene : n_gene + n_var],
        packed[:, n_cov, n_gene : n_gene + n_var],
    )
    gram, counts = packed[:, :n_cov, n_gene + n_var :], packed[:, n_cov, n_gene + n_var]
    inverse = invert(gram)
    pa = jnp.einsum("tkj,tjv->tkv", inverse, amat, precision=HIGHEST)
    pb = jnp.einsum("tkj,tjg->tkg", inverse, bmat, precision=HIGHEST)
    gnorm = gsq - jnp.sum(amat * pa, axis=1)
    enorm = esq - jnp.sum(bmat * pb, axis=1)
    live_f = live.astype(jnp.float32)
    live_own = lax.dynamic_slice_in_dim(live_f, ix * tis_dev, tis_dev, 0)
    scales = live_own * jnp.sqrt(jnp.maximum(counts - n_cov, 1.0))
    inv_var = 1.0 / jnp.sqrt(gnorm + 1e-05)
    inv_gene = scales[:, None] / jnp.sqrt(enorm + 1e-05)
    gres = dos_m - jnp.einsum("tks,tkv->tsv", cov_m, pa, precision=HIGHEST)
    gres = (gres * inv_var[:, None, :]).astype(jnp.bfloat16)
    eres = exp_m - jnp.einsum("tks,tkg->tsg", cov_m, pb, precision=HIGHEST)
    eres = (eres * inv_gene[:, None, :]).astype(jnp.bfloat16)
    half = (n_v // n_s) * n_var // n_x
    kept, got = [], []
    for start, stop in zip(CUTS, CUTS[1:]):
        low, high = tis_dev * start // CUTS[-1], tis_dev * stop // CUTS[-1]
        chunk = cross_chunk(gres[low:high], eres[low:high], n_s, n_v, i_s, i_v)
        kept.append(lax.dynamic_slice_in_dim(chunk, ix * half, half, 1))
        sent = lax.dynamic_slice_in_dim(chunk, (n_x - 1 - ix) * half, half, 1)
        got.append(lax.ppermute(sent, "tissue", [(0, 1), (1, 0)]))
    mix_own = lax.dynamic_slice_in_dim(mixing, ix * tis_dev, tis_dev, 1)
    mix_far = lax.dynamic_slice_in_dim(mixing, (n_x - 1 - ix) * tis_dev, tis_dev, 1)
    yvals = jnp.einsum(
        "ut,tvg->uvg",
        jnp.concatenate([mix_own, mix_far], axis=1) * live_f[:, None],
        jnp.concatenate(kept + got, axis=0).astype(jnp.float32),
        precision=HIGHEST,
    )
    nlive = jnp.maximum(jnp.sum(live_f), 1.0)
    stats = jnp.stack(
        [jnp.sum(yvals * yvals, axis=0) / nlive, jnp.sum(yvals, axis=0) / jnp.sqrt(nlive)]
    ).astype(jnp.bfloat16)
    if n_s == n_v:
        near, far = [], []
        for x in range(n_x):
            for i in range(n_s):
                for j in range(n_v):
                    source = (x * n_s + i) * n_v + j
                    near.append((source, (x * n_s + j) * n_v + i))
                    far.append((source, ((n_x - 1 - x) * n_s + j) * n_v + i))
        axes = ("tissue", "sample", "variant")
        one = lax.ppermute(stats, axes, near)
        two = lax.ppermute(stats, axes, far)
        full = jnp.concatenate(
            [jnp.where(ix == 0, one, two), jnp.where(ix == 0, two, one)], axis=1
        )
    else:
        blocks = lax.all_gather(stats, ("tissue", "sample", "variant"), axis=0)
        blocks = blocks.reshape((n_x, n_s, n_v) + stats.shape)
        blocks = jnp.transpose(blocks, (3, 1, 0, 4, 2, 5))
        whole = blocks.reshape(2, n_v * n_var, n_v * n_gene)
        genes = whole.shape[2] // n_s
        full = lax.dynamic_slice(whole, (0, i_v * n_var, i_s * genes), (2, n_var, genes))
    full = full.astype(jnp.float32)
    return (full[0], full[1])


def solution(mesh):
    return jax.shard_map(
        body,
        mesh=mesh,
        in_specs=(
            P("tissue", "sample", "variant"),
            P("tissue", "sample", "variant"),
            P("tissue", None, "sample"),
            P("tissue", "sample"),
            P(),
            P(),
        ),
        out_specs=(P("variant", "sample"), P("variant", "sample")),
        check_vma=False,
    )
```

```python
import jax
import jax.numpy as jnp
from jax import lax
from jax.experimental import pallas as pl
from jax.experimental.pallas import tpu as pltpu
from jax.sharding import PartitionSpec as P

HIGHEST = lax.Precision.HIGHEST
CUTS = (0, 8, 17, 26)


def invert_kernel(gram_ref, out_ref):
    n = gram_ref.shape[0]
    lanes = gram_ref.shape[2]
    eye = (
        lax.broadcasted_iota(jnp.int32, (n, n, lanes), 0)
        == lax.broadcasted_iota(jnp.int32, (n, n, lanes), 1)
    ).astype(jnp.float32)
    out_ref[...] = gram_ref[...] + eye
    row_ids = lax.broadcasted_iota(jnp.int32, (n, lanes), 0)

    def step(k, carry):
        pivot = 1.0 / out_ref[k, pl.ds(k, 1), :]
        here = row_ids == k
        row = jnp.where(here, pivot, out_ref[k] * pivot)
        col = out_ref[:, pl.ds(k, 1), :]
        out_ref[...] = jnp.where(here[None], 0.0, out_ref[...]) - col * row[None]
        out_ref[k] = row
        return carry

    lax.fori_loop(0, n, step, 0)


def invert(gram):
    tis, n, _ = gram.shape
    lanes = -(-tis // 128) * 128
    packed = jnp.pad(jnp.transpose(gram, (1, 2, 0)), ((0, 0), (0, 0), (0, lanes - tis)))
    out = pl.pallas_call(
        invert_kernel,
        out_shape=jax.ShapeDtypeStruct((n, n, lanes), jnp.float32),
        name="invert_gram",
    )(packed)
    return jnp.transpose(out[:, :, :tis], (2, 0, 1))


def swap(value, bit, n_s):
    return lax.ppermute(value, "sample", [(i, i ^ bit) for i in range(n_s)])


def add(first, second):
    return (first.astype(jnp.float32) + second.astype(jnp.float32)).astype(jnp.bfloat16)


def sum_over_samples(value, n_s, i_s):
    half = value.shape[0] // 2
    odd = i_s % 2
    mine = lax.dynamic_slice_in_dim(value, odd * half, half, 0)
    sent = lax.dynamic_slice_in_dim(value, (1 - odd) * half, half, 0)
    mine = add(mine, swap(sent, 1, n_s))
    bit = 2
    while bit < n_s:
        mine = add(mine, swap(mine, bit, n_s))
        bit *= 2
    other = swap(mine, 1, n_s)
    return jnp.concatenate(
        [jnp.where(odd == 0, mine, other), jnp.where(odd == 0, other, mine)], axis=0
    )


def cross_chunk(gres, eres, n_s, n_v, i_s, i_v, hold):
    if n_v == n_s:
        gathered = jnp.stack(
            [gres]
            + [
                lax.ppermute(gres, "variant", [(j, j ^ shift) for j in range(n_v)])
                for shift in range(1, n_v)
            ]
        )
        first = i_v
    else:
        gathered = lax.all_gather(gres, "variant", axis=0)
        first = 0
    if hold is not None:
        gathered, _ = lax.optimization_barrier((gathered, hold))
    per = n_v // n_s
    blocks = {}
    for offset in reversed(range(n_s)):
        pieces = [
            jnp.einsum(
                "tsv,tsg->tvg",
                lax.dynamic_index_in_dim(gathered, ((i_s ^ offset) * per + m) ^ first, 0, False),
                eres,
                preferred_element_type=jnp.float32,
            ).astype(jnp.bfloat16)
            for m in range(per)
        ]
        blocks[offset] = pieces[0] if per == 1 else jnp.concatenate(pieces, axis=1)
    bit = 1
    while bit < n_s:
        for offset in [o for o in blocks if o & bit]:
            arrived = swap(blocks.pop(offset), bit, n_s)
            blocks[offset ^ bit] = add(blocks[offset ^ bit], arrived)
        if bit == 1:
            hold = blocks[max(blocks)]
        bit *= 2
    return blocks[0], hold


def body(dosage, express, covar, member, live, mixing):
    tis_dev = dosage.shape[0]
    n_cov = covar.shape[1]
    n_x = lax.axis_size("tissue")
    n_s = lax.axis_size("sample")
    n_v = lax.axis_size("variant")
    ix = lax.axis_index("tissue")
    i_s = lax.axis_index("sample")
    i_v = lax.axis_index("variant")
    weights = member.astype(jnp.float32)
    dos_m = dosage.astype(jnp.float32) * weights[:, :, None]
    cov_m = covar * weights[:, None, :]
    exp_m = express.astype(jnp.float32) * weights[:, :, None]
    gram = jnp.einsum("tks,tjs->tkj", cov_m, cov_m, precision=HIGHEST)
    amat = jnp.einsum("tks,tsv->tkv", cov_m, dos_m, precision=HIGHEST)
    bmat = jnp.einsum("tks,tsg->tkg", cov_m, exp_m, precision=HIGHEST)
    gsq = jnp.sum(dos_m * dos_m, axis=1)
    esq = jnp.sum(exp_m * exp_m, axis=1)
    counts = jnp.sum(weights, axis=1)
    n_var, n_gene = dosage.shape[2], express.shape[2]
    count_row = jnp.pad(counts[:, None], ((0, 0), (0, n_cov - 1)))
    packed = jnp.concatenate(
        [
            jnp.concatenate([bmat, amat, gram], axis=2).astype(jnp.bfloat16),
            jnp.concatenate([esq, gsq, count_row], axis=1).astype(jnp.bfloat16)[:, None],
        ],
        axis=1,
    )
    packed = sum_over_samples(packed, n_s, i_s).astype(jnp.float32)
    bmat, esq = packed[:, :n_cov, :n_gene], packed[:, n_cov, :n_gene]
    amat, gsq = (
        packed[:, :n_cov, n_gene : n_gene + n_var],
        packed[:, n_cov, n_gene : n_gene + n_var],
    )
    gram, counts = packed[:, :n_cov, n_gene + n_var :], packed[:, n_cov, n_gene + n_var]
    inverse = invert(gram)
    pa = jnp.einsum("tkj,tjv->tkv", inverse, amat, precision=HIGHEST)
    pb = jnp.einsum("tkj,tjg->tkg", inverse, bmat, precision=HIGHEST)
    gnorm = gsq - jnp.sum(amat * pa, axis=1)
    enorm = esq - jnp.sum(bmat * pb, axis=1)
    live_f = live.astype(jnp.float32)
    live_own = lax.dynamic_slice_in_dim(live_f, ix * tis_dev, tis_dev, 0)
    scales = live_own * jnp.sqrt(jnp.maximum(counts - n_cov, 1.0))
    inv_var = 1.0 / jnp.sqrt(gnorm + 1e-05)
    inv_gene = scales[:, None] / jnp.sqrt(enorm + 1e-05)
    gres = dos_m - jnp.einsum("tks,tkv->tsv", cov_m, pa, precision=HIGHEST)
    gres = (gres * inv_var[:, None, :]).astype(jnp.bfloat16)
    eres = exp_m - jnp.einsum("tks,tkg->tsg", cov_m, pb, precision=HIGHEST)
    eres = (eres * inv_gene[:, None, :]).astype(jnp.bfloat16)
    half = (n_v // n_s) * n_var // n_x
    kept, got, hold = [], [], None
    for start, stop in zip(CUTS, CUTS[1:]):
        low, high = tis_dev * start // CUTS[-1], tis_dev * stop // CUTS[-1]
        chunk, hold = cross_chunk(
            gres[low:high], eres[low:high], n_s, n_v, i_s, i_v, hold
        )
        kept.append(lax.dynamic_slice_in_dim(chunk, ix * half, half, 1))
        sent = lax.dynamic_slice_in_dim(chunk, (n_x - 1 - ix) * half, half, 1)
        got.append(lax.ppermute(sent, "tissue", [(0, 1), (1, 0)]))
    mix_own = lax.dynamic_slice_in_dim(mixing, ix * tis_dev, tis_dev, 1)
    mix_far = lax.dynamic_slice_in_dim(mixing, (n_x - 1 - ix) * tis_dev, tis_dev, 1)
    yvals = jnp.einsum(
        "ut,tvg->uvg",
        jnp.concatenate([mix_own, mix_far], axis=1) * live_f[:, None],
        jnp.concatenate(kept + got, axis=0).astype(jnp.float32),
        precision=HIGHEST,
    )
    nlive = jnp.maximum(jnp.sum(live_f), 1.0)
    stats = jnp.stack(
        [jnp.sum(yvals * yvals, axis=0) / nlive, jnp.sum(yvals, axis=0) / jnp.sqrt(nlive)]
    ).astype(jnp.bfloat16)
    if n_s == n_v:
        near, far = [], []
        for x in range(n_x):
            for i in range(n_s):
                for j in range(n_v):
                    source = (x * n_s + i) * n_v + j
                    near.append((source, (x * n_s + j) * n_v + i))
                    far.append((source, ((n_x - 1 - x) * n_s + j) * n_v + i))
        axes = ("tissue", "sample", "variant")
        one = lax.ppermute(stats, axes, near)
        two = lax.ppermute(stats, axes, far)
        full = jnp.concatenate(
            [jnp.where(ix == 0, one, two), jnp.where(ix == 0, two, one)], axis=1
        )
    else:
        blocks = lax.all_gather(stats, ("tissue", "sample", "variant"), axis=0)
        blocks = blocks.reshape((n_x, n_s, n_v) + stats.shape)
        blocks = jnp.transpose(blocks, (3, 1, 0, 4, 2, 5))
        whole = blocks.reshape(2, n_v * n_var, n_v * n_gene)
        genes = whole.shape[2] // n_s
        full = lax.dynamic_slice(whole, (0, i_v * n_var, i_s * genes), (2, n_var, genes))
    full = full.astype(jnp.float32)
    return (full[0], full[1])


def solution(mesh):
    return jax.shard_map(
        body,
        mesh=mesh,
        in_specs=(
            P("tissue", "sample", "variant"),
            P("tissue", "sample", "variant"),
            P("tissue", None, "sample"),
            P("tissue", "sample"),
            P(),
            P(),
        ),
        out_specs=(P("variant", "sample"), P("variant", "sample")),
        check_vma=False,
    )
```
